128 devices in a mesh: branch: 2 (over core), group: 2 (over y_hi), seq: 32 (over y_lo, x, z).
Axes of the slice: x: 4, y: 4 (y_hi: 2, y_lo: 2; y = y_hi * 2 + y_lo), z: 4, core: 2. Of those that a mesh axis runs over, the one named last changes fastest.
Arguments:
- query_rows: bfloat16 [2, 10240, 4096], P('branch', ('group', 'seq')), parts along dimension 1, may hold values from -10 to 10
- key_rows: bfloat16 [2, 10240, 4096], P('branch', ('group', 'seq')), parts along dimension 1, may hold values from -9 to 9
- value_rows: bfloat16 [2, 10240, 4096], P('branch', ('group', 'seq')), parts along dimension 1, may hold values from -80 to 80
- residual: bfloat16 [10240, 2560], P(('group', 'seq')), parts along dimension 0, may hold values from -6 to 6
- control_mask: int32 [10240], P(('group', 'seq')), parts along dimension 0, may hold values 0 or 1
- step_index: int32 [2], P('group'), parts along dimension 0, may hold values from 0 to 49
- step_gates: float32 [50, 2560], replicated, may hold values from 0.1 to 1.9
- out_weight: bfloat16 [2, 4096, 2560], P('branch', None, 'seq'), may hold values from -0.21875 to 0.21875
Outputs:
- block_out: bfloat16 [2, 10240, 2560], P('branch', ('group', 'seq')), parts along dimension 1
The draws below stay inside these ranges and needn't reach their ends.
There are 2 independent parts, one for each index of `group`. The reference program is written for one: setup_inputs(seed, part) draws one part's arguments, and reference() takes and returns one part's arrays. A program takes and returns all parts, laid end to end along the dimension named above; an argument that names none is the same for every part. Nothing has to cross between parts.
All inputs are finite; a program needn't handle non-finite values. No bound on the sum of `control_mask` on one device may be relied on, other than what follows from the above.
Results may differ from the reference program's by a relative error of at most 0.007.
Values may be sent and summed in bfloat16 or wider, within the bound.
A program may use at most 128 MiB of HBM per device.

```python
import jax
import jax.numpy as jnp
from jax import lax

HEADS = 32
DH = 128
DW = 2560
STEPS = 50
HF = 4096
TOKENS = 5120


def base_field(key, shape):
    return jax.random.normal(key, shape, jnp.float32)


def draw_query_rows(key, part):
    drawn = jnp.clip(2.0 * base_field(jax.random.fold_in(key, 1), (2, TOKENS, HEADS, DH)), -9.0, 9.0)
    return drawn.reshape(2, TOKENS, HEADS * DH).astype(jnp.bfloat16)


def draw_key_rows(key, part):
    drawn = jnp.clip(base_field(jax.random.fold_in(key, 2), (2, TOKENS, HEADS, DH)), -9.0, 9.0)
    return drawn.reshape(2, TOKENS, HEADS * DH).astype(jnp.bfloat16)


def draw_value_rows(key, part):
    row_scale = 10.0 ** jax.random.uniform(jax.random.fold_in(key, 3), (2, TOKENS, 1), jnp.float32, 0.0, 1.0)
    noise = jnp.clip(base_field(jax.random.fold_in(key, 4), (2, TOKENS, HEADS * DH)), -6.0, 6.0)
    field = row_scale * noise
    return field.astype(jnp.bfloat16)


def place_ends(values, rng, least, high):
    longest = values.shape.index(max(values.shape))
    spots = []
    for shift in (0, 1):
        where = [jax.random.randint(jax.random.fold_in(rng, axis), (), 0, length) for axis, length in enumerate(values.shape)]
        where[longest] = (where[longest] + shift) % values.shape[longest]
        spots.append(tuple(where))
    return values.at[spots[0]].set(least).at[spots[1]].set(high)


def block_levels(rng, dims, split, least, high):
    def one(axis_at, blocks):
        heights = jax.random.uniform(jax.random.fold_in(jax.random.fold_in(rng, 6), axis_at), (blocks,), jnp.float32, least / len(split), high / len(split))
        return jnp.repeat(jnp.exp(heights), dims[axis_at] // blocks).reshape((-1,) + (1,) * (len(dims) - axis_at - 1))

    level = one(*split[0])
    for cut in split[1:]:
        level = level * one(*cut)
    return level


def centred(own_key, shape, spread, limit, cuts=(), held_as=jnp.bfloat16):
    array = jax.random.normal(own_key, shape, jnp.float32) * spread
    if len(cuts) > 0:
        array = block_levels(own_key, shape, cuts, -0.22, 0.18) * array
    return jnp.clip(array, min=-limit, max=limit).astype(held_as)


def setup_inputs(seed: int = 0, part: int = 0) -> dict:
    keys = jax.random.split(jax.random.key(seed), 9)
    part_splits = jax.random.split(jax.random.fold_in(keys[8], part), 9)
    query_rows = draw_query_rows(jax.random.fold_in(jax.random.fold_in(keys[8], part), 71), part)
    key_rows = draw_key_rows(jax.random.fold_in(jax.random.fold_in(keys[8], part), 71), part)
    value_rows = draw_value_rows(jax.random.fold_in(jax.random.fold_in(keys[8], part), 71), part)
    residual = centred(part_splits[3], (TOKENS, DW), 1.0, 6.0, ((0, 32),))
    control_mask = place_ends((jax.random.randint(part_splits[4], (TOKENS,), 0, 4) < 3).astype(jnp.int32), jax.random.fold_in(part_splits[4], 1), 0, 1)
    step_index = jax.random.randint(part_splits[5], (1,), 0, STEPS).astype(jnp.int32)
    step_gates = jnp.clip(1.0 + 0.18 * jax.random.normal(keys[6], (STEPS, DW), jnp.float32), 0.1, 1.9)
    out_weight = centred(keys[7], (2, HF, DW), (HF * 1024 // TOKENS) ** -0.5, 0.21875, ((0, 2), (2, 32)))
    return dict(query_rows=query_rows, key_rows=key_rows, value_rows=value_rows, residual=residual, control_mask=control_mask, step_index=step_index, step_gates=step_gates, out_weight=out_weight)


def head_attention(query_head, key_head, value_head):
    score_scale = float(DH) ** -0.5
    scores = jnp.dot(query_head, key_head.T, preferred_element_type=jnp.float32) * score_scale
    peak = jnp.max(scores, axis=1, keepdims=True)
    expo = jnp.exp(scores - peak)
    total_sum = jnp.sum(expo, axis=1, keepdims=True)
    probs = expo.astype(jnp.bfloat16)
    attended = jnp.dot(probs, value_head, preferred_element_type=jnp.float32) / total_sum
    return attended.astype(jnp.bfloat16)


def branch_projection(query_all, key_all, value_all, weight_matrix):
    query_heads = query_all.reshape(TOKENS, HEADS, DH).transpose(1, 0, 2)
    key_heads = key_all.reshape(TOKENS, HEADS, DH).transpose(1, 0, 2)
    value_heads = value_all.reshape(TOKENS, HEADS, DH).transpose(1, 0, 2)
    attended = lax.map(lambda triple: head_attention(triple[0], triple[1], triple[2]), (query_heads, key_heads, value_heads))
    attended = attended.transpose(1, 0, 2).reshape(TOKENS, HEADS * DH)
    return jnp.dot(attended, weight_matrix, preferred_element_type=jnp.float32)


def reference(query_rows, key_rows, value_rows, residual, control_mask, step_index, step_gates, out_weight):
    context_proj = branch_projection(query_rows[0], key_rows[0], value_rows[0], out_weight[0])
    main_proj = branch_projection(query_rows[1], key_rows[1], value_rows[1], out_weight[1])
    hints = jnp.where(control_mask[:, None] == 1, context_proj, jnp.zeros_like(context_proj)).astype(jnp.bfloat16)
    gate_row = lax.dynamic_slice_in_dim(step_gates, step_index[0].astype(jnp.int32), 1, 0)[0]
    mixed_out = residual.astype(jnp.float32) + gate_row[None, :] * main_proj + hints.astype(jnp.float32)
    return jnp.stack([hints, mixed_out.astype(jnp.bfloat16)])
```

```python
import math

import jax
import jax.numpy as jnp
from jax import lax
from jax.experimental import pallas as pl
from jax.experimental.pallas import tpu as pltpu
from jax.sharding import PartitionSpec as P

HEADS = 32
DH = 128
NX = 4
NZ = 4
PLANE = NX * NZ
SEQ = 2 * PLANE
MESH = pl.DeviceIdType.MESH
KEY_CHUNK = 512
OUT_CHUNK = 512
NT = (((1,), (1,)), ((), ()))


def shifted(value, axis, steps):
    count = lax.axis_size(axis)
    leading, last = (max(0, -steps), min(count, count - steps))
    return lax.ppermute(value, axis, [(source, source + steps) for source in range(leading, last)])


def fused_kernel(
    q_hbm, k_hbm, v_hbm, wt_hbm, out_ref,
    q_s, k_s, v_s, s_a, s_b, m_a, m_b, o_s, att, wg, own, sbuf, rbuf,
    qkv_send, qkv_recv, local_sem, w_send, w_recv, a_send, a_recv, r_send, r_recv,
):
    rows = q_hbm.shape[1]
    half = wt_hbm.shape[1] // 2
    cols = wt_hbm.shape[0]
    keys = k_s.shape[0]
    block = 2 * rows
    factor = float(DH) ** -0.5 * math.log2(math.e)
    me = lax.axis_index("seq")
    y = me // PLANE
    x = (me // NZ) % NX
    z = me % NZ

    def index(yy, xx, zz):
        return yy * PLANE + ((xx + NX) % NX) * NZ + (zz + NZ) % NZ

    def aligned(value, step):
        return pl.ds(pl.multiple_of(value * step, step), step)

    def q_slot(source):
        return q_s.at[aligned((source % PLANE) * 2 + source // PLANE, rows)]

    def k_slot(source):
        return k_s.at[aligned(source, rows)]

    def v_slot(source):
        return v_s.at[aligned(source, rows), pl.ds(0, DH)]

    streams = ((q_hbm, q_slot), (k_hbm, k_slot), (v_hbm, v_slot))

    def head_of(hbm, head):
        return hbm.at[0, :, aligned(head, DH)]

    def qkv_copy(number, peer, source):
        hbm, slot = streams[number]
        return pltpu.make_async_remote_copy(
            src_ref=head_of(hbm, peer), dst_ref=slot(source),
            send_sem=qkv_send.at[number, peer], recv_sem=qkv_recv.at[number, source],
            device_id={"seq": peer}, device_id_type=MESH,
        )

    def w_slot(source):
        return wg.at[aligned(source, cols)]

    def w_copy(slot, peer, number):
        return pltpu.make_async_remote_copy(
            src_ref=w_slot(slot), dst_ref=w_slot(slot),
            send_sem=w_send.at[number], recv_sem=w_recv.at[slot],
            device_id={"seq": peer}, device_id_type=MESH,
        )

    def w_wait(slot):
        w_copy(slot, me, 0).wait_recv()

    own_copies = [
        pltpu.make_async_copy(head_of(hbm, me), slot(me), local_sem.at[n])
        for n, (hbm, slot) in enumerate(streams)
    ]
    own_w = pltpu.make_async_copy(wt_hbm.at[:, aligned(y, half)], w_slot(me), local_sem.at[3])
    for copy in own_copies:
        copy.start()
    own_w.start()

    barrier = pltpu.get_barrier_semaphore()

    @pl.loop(1, SEQ)
    def _(k):
        pl.semaphore_signal(
            barrier, inc=1, device_id={"seq": (me + k) % SEQ}, device_id_type=MESH
        )

    pl.semaphore_wait(barrier, SEQ - 1)

    def peer_at(k):
        return ((y + k // PLANE) % 2) * PLANE + ((x + k // NZ) % NX) * NZ + (z + k) % NZ

    for number in range(3):
        @pl.loop(1, SEQ)
        def _(k):
            qkv_copy(number, peer_at(k), me).start()

    partner = (1 - y) * PLANE + x * NZ + z
    w_first = pltpu.make_async_remote_copy(
        src_ref=wt_hbm.at[:, aligned(1 - y, half)], dst_ref=w_slot(me),
        send_sem=w_send.at[0], recv_sem=w_recv.at[me],
        device_id={"seq": partner}, device_id_type=MESH,
    )
    w_first.start()
    v_s[:, DH:] = jnp.ones((keys, DH), jnp.bfloat16)

    def send_w(slot, peer, number):
        w_copy(slot, peer, number).start()

    def flow(kind, along, across):
        return (index(0, x + along, z + across) if kind == 0 else index(1, x + across, z + along))

    def first_peer(kind, step):
        return index(y, x + step, z) if kind == 0 else index(y, x, z + step)

    def second_peer(kind, step):
        return index(y, x, z + step) if kind == 0 else index(y, x + step, z)

    def stage_one():
        for kind in range(2):
            for at, step in enumerate((1, -1, 2)):
                send_w(flow(kind, 0, 0), first_peer(kind, step), 1 + 3 * kind + at)
        for kind in range(2):
            for at, step in enumerate((1, -1)):
                send_w(flow(kind, 0, 0), second_peer(kind, step), 7 + 2 * kind + at)

    def stage_two(along):
        for kind in range(2):
            w_wait(flow(kind, along, 0))
            for at, step in enumerate((1, -1)):
                number = 11 + 4 * (along % NX - 1) + 2 * kind + at
                send_w(flow(kind, along, 0), second_peer(kind, step), number)

    def stage_three(along, step):
        for kind in range(2):
            w_wait(flow(kind, along, -step))
            number = 23 + 2 * (along % NX) + kind
            send_w(flow(kind, along, -step), second_peer(kind, step), number)

    events = {
        3: lambda: stage_two(1),
        4: lambda: stage_two(-1),
        5: lambda: stage_two(2),
        6: lambda: stage_three(0, 1),
        8: lambda: stage_three(1, 1),
        10: lambda: stage_three(-1, -1),
        12: lambda: stage_three(2, -1),
    }

    for number in range(3):
        own_copies[number].wait()

        @pl.loop(1, SEQ)
        def _(k):
            qkv_copy(number, me, (me + k) % SEQ).wait_recv()

    own_w.wait()
    w_wait(partner)
    stage_one()

    def shift_of(step):
        left = PLANE - 1 - step
        return left // NZ, left % NZ

    def plane_at(step):
        dx, dz = shift_of(step)
        return ((x + dx) % NX) * NZ + (z + dz) % NZ

    def attend(step, now, following):
        lanes = KEY_CHUNK // DH
        if following is not None:
            scores_ref, peak_ref = following
            query = q_s[aligned(plane_at(step + 1), block), :]
            peak = None
        if now is not None:
            held_ref, held_peak = now
            total = jnp.zeros((block, 2 * DH), jnp.float32)
        for chunk in range(keys // KEY_CHUNK):
            span = pl.ds(chunk * KEY_CHUNK, KEY_CHUNK)
            if following is not None:
                scores = lax.dot_general(
                    query, k_s[span, :], NT, preferred_element_type=jnp.float32
                )
                scores_ref[:, span] = scores
                for lane in range(lanes):
                    piece = scores[:, lane * DH : (lane + 1) * DH]
                    peak = piece if peak is None else jnp.maximum(peak, piece)
            if now is not None:
                shift = held_peak[...]
                probs = [
                    jnp.exp2(
                        held_ref[:, pl.ds(chunk * KEY_CHUNK + lane * DH, DH)] * factor - shift
                    ).astype(jnp.bfloat16)
                    for lane in range(lanes)
                ]
                total += jnp.dot(
                    jnp.concatenate(probs, axis=1), v_s[span, :],
                    preferred_element_type=jnp.float32,
                )
        if following is not None:
            top = jnp.max(peak, axis=1, keepdims=True) * factor
            peak_ref[...] = jnp.broadcast_to(top, (block, DH))
        if now is not None:
            o_s[step] = (total[:, :DH] / total[:, DH:]).astype(jnp.bfloat16)

    my_plane = x * NZ + z

    def a_copy(step, plane, source):
        return pltpu.make_async_remote_copy(
            src_ref=o_s.at[step], dst_ref=att.at[:, aligned(source, DH)],
            send_sem=a_send.at[step], recv_sem=a_recv.at[source],
            device_id={"seq": y * PLANE + plane}, device_id_type=MESH,
        )

    first, second = (s_a, m_a), (s_b, m_b)
    attend(-1, None, first)

    @pl.loop(0, PLANE // 2 - 1)
    def _(pair):
        for part in range(2):
            step = pair * 2 + part
            for at, event in events.items():
                if at % 2 == part:
                    pl.when(pair == at // 2)(event)
            attend(step, (first, second)[part], (second, first)[part])
            a_copy(step, plane_at(step), my_plane).start()

    attend(PLANE - 2, first, second)
    a_copy(PLANE - 2, plane_at(PLANE - 2), my_plane).start()
    attend(PLANE - 1, second, None)
    own_a = pltpu.make_async_copy(
        o_s.at[PLANE - 1], att.at[:, aligned(my_plane, DH)], local_sem.at[4]
    )
    own_a.start()

    for kind in range(2):
        for along, across in ((-1, -1), (2, -1), (0, 1), (1, 1), (0, 2), (1, 2), (-1, 2), (2, 2)):
            w_wait(flow(kind, along, across))

    @pl.loop(1, PLANE)
    def _(k):
        a_copy(0, my_plane, (my_plane + k) % PLANE).wait_recv()

    own_a.wait()

    def r_copy(chunk):
        return pltpu.make_async_remote_copy(
            src_ref=sbuf.at[chunk], dst_ref=rbuf.at[chunk],
            send_sem=r_send.at[chunk], recv_sem=r_recv.at[chunk],
            device_id={"seq": partner}, device_id_type=MESH,
        )

    chunks = sbuf.shape[0]

    @pl.loop(0, chunks)
    def _(chunk):
        weights = wg[aligned(chunk, OUT_CHUNK), :]
        sbuf[chunk] = lax.dot_general(
            att[aligned(1 - y, rows), :], weights, NT, preferred_element_type=jnp.float32
        ).astype(jnp.bfloat16)
        own[chunk] = lax.dot_general(
            att[aligned(y, rows), :], weights, NT, preferred_element_type=jnp.float32
        )
        r_copy(chunk).start()

    for chunk in range(chunks):
        r_copy(chunk).wait_recv()
        out_ref[:, chunk * OUT_CHUNK : (chunk + 1) * OUT_CHUNK] = own[chunk] + rbuf[
            chunk
        ].astype(jnp.float32)

    for number in range(3):
        @pl.loop(1, SEQ)
        def _(k):
            qkv_copy(number, (me + k) % SEQ, me).wait_send()

    w_first.wait_send()
    for number in range(1, SEQ - 1):
        w_copy(0, me, number).wait_send()

    @pl.loop(0, PLANE - 1)
    def _(step):
        a_copy(step, my_plane, my_plane).wait_send()

    for chunk in range(chunks):
        r_copy(chunk).wait_send()


def per_device(
    query_rows, key_rows, value_rows, residual, control_mask, step_index, step_gates, out_weight
):
    rows = query_rows.shape[1]
    tokens = rows * SEQ
    block = 2 * rows
    width = residual.shape[1]
    features = out_weight.shape[1]
    chunks = width // OUT_CHUNK
    weight_rows = jnp.swapaxes(out_weight[0], 0, 1)
    bf16, f32 = jnp.bfloat16, jnp.float32
    projected = pl.pallas_call(
        fused_kernel,
        out_shape=jax.ShapeDtypeStruct((rows, width), f32),
        in_specs=[pl.BlockSpec(memory_space=pl.ANY)] * 4,
        out_specs=pl.BlockSpec(memory_space=pltpu.VMEM),
        scratch_shapes=[
            pltpu.VMEM((tokens, DH), bf16),
            pltpu.VMEM((tokens, DH), bf16),
            pltpu.VMEM((tokens, 2 * DH), bf16),
            pltpu.VMEM((block, tokens), f32),
            pltpu.VMEM((block, tokens), f32),
            pltpu.VMEM((block, DH), f32),
            pltpu.VMEM((block, DH), f32),
            pltpu.VMEM((PLANE, block, DH), bf16),
            pltpu.VMEM((block, features // 2), bf16),
            pltpu.VMEM((width, features // 2), bf16),
            pltpu.VMEM((chunks, rows, OUT_CHUNK), f32),
            pltpu.VMEM((chunks, rows, OUT_CHUNK), bf16),
            pltpu.VMEM((chunks, rows, OUT_CHUNK), bf16),
            pltpu.SemaphoreType.DMA((3, SEQ)),
            pltpu.SemaphoreType.DMA((3, SEQ)),
            pltpu.SemaphoreType.DMA((5,)),
            pltpu.SemaphoreType.DMA((SEQ,)),
            pltpu.SemaphoreType.DMA((SEQ,)),
            pltpu.SemaphoreType.DMA((PLANE,)),
            pltpu.SemaphoreType.DMA((PLANE,)),
            pltpu.SemaphoreType.DMA((chunks,)),
            pltpu.SemaphoreType.DMA((chunks,)),
        ],
        compiler_params=pltpu.CompilerParams(
            collective_id=0, has_side_effects=True, vmem_limit_bytes=60000 * 1024
        ),
        name="attend_project",
    )(query_rows, key_rows, value_rows, weight_rows)
    hint_local = jnp.where(control_mask[:, None] == 1, projected, jnp.zeros_like(projected)).astype(
        jnp.bfloat16
    )
    hint_moved = shifted(hint_local, "branch", 1)
    step_ids = lax.broadcasted_iota(jnp.int32, (step_gates.shape[0], 1), 0)
    gate_row = jnp.sum(
        jnp.where(step_ids == step_index[0], step_gates, jnp.zeros_like(step_gates)), axis=0
    )
    mixed_out = (
        residual.astype(jnp.float32)
        + gate_row[None, :] * projected
        + hint_moved.astype(jnp.float32)
    )
    is_main = lax.axis_index("branch") == 1
    chosen_out = jnp.where(is_main, mixed_out.astype(jnp.bfloat16), hint_local)
    return chosen_out[None]


def solution(mesh):
    placed = (
        P("branch", ("group", "seq"), None),
        P("branch", ("group", "seq"), None),
        P("branch", ("group", "seq"), None),
        P(("group", "seq"), None),
        P(("group", "seq")),
        P("group"),
        P(),
        P("branch", None, "seq"),
    )
    return jax.shard_map(
        per_device,
        mesh=mesh,
        in_specs=placed,
        out_specs=P("branch", ("group", "seq"), None),
        check_vma=False,
    )
```

```python
import math

import jax
import jax.numpy as jnp
from jax import lax
from jax.experimental import pallas as pl
from jax.experimental.pallas import tpu as pltpu
from jax.sharding import PartitionSpec as P

DH = 128
NX = 4
NZ = 4
PLANE = NX * NZ
SEQ = 2 * PLANE
MESH = pl.DeviceIdType.MESH
KEY_CHUNK = 512
SPREAD_LAG = 2
RELAY_LAG = 4
W_STEPS = (5, 6, 7, 8, 9, 10, 11, 12, 12, 13)
NT = (((1,), (1,)), ((), ()))


def fused_kernel(
    index_ref, q_hbm, k_hbm, v_hbm, wt_hbm, res_hbm, mask_hbm, gates_hbm, out_ref,
    q_s, k_s, v_s, s_a, s_b, m_a, m_b, o_s, att, wg, sbuf, rbuf, hints, res_s, mask_s, gates_s,
    qkv_send, qkv_recv, local_sem, w_send, w_recv, a_send, a_recv, f_send, g_send,
    r_send, r_recv, h_send, h_recv,
):
    rows = q_hbm.shape[1]
    cols = wt_hbm.shape[0]
    keys = k_s.shape[0]
    block = 2 * rows
    steps = keys // block
    wide = rbuf.shape[3]
    quarter = wt_hbm.shape[1] // 4
    factor = float(DH) ** -0.5 * math.log2(math.e)
    branch = lax.axis_index("branch")
    me = lax.axis_index("seq")
    y = me // PLANE
    x = (me // NZ) % NX
    z = me % NZ

    def index(yy, xx, zz):
        return (yy % 2) * PLANE + ((xx + NX) % NX) * NZ + (zz + NZ) % NZ

    def aligned(value, step):
        return pl.ds(pl.multiple_of(value * step, step), step)

    def q_slot(source):
        order = ((source // PLANE) * NZ + source % NZ) * NX + (source // NZ) % NX
        return q_s.at[aligned(order, rows)]

    def k_slot(source):
        return k_s.at[aligned(source, rows)]

    def v_slot(source):
        return v_s.at[aligned(source, rows), pl.ds(0, DH)]

    streams = ((q_hbm, q_slot), (k_hbm, k_slot), (v_hbm, v_slot))

    def head_of(hbm, head):
        return hbm.at[0, :, aligned(head, DH)]

    def qkv_copy(number, peer, source):
        hbm, slot = streams[number]
        return pltpu.make_async_remote_copy(
            src_ref=head_of(hbm, peer), dst_ref=slot(source),
            send_sem=qkv_send.at[number, peer], recv_sem=qkv_recv.at[number, source],
            device_id={"seq": peer}, device_id_type=MESH,
        )

    def w_slot(yy, zz):
        start = (yy % 2) * wide + (x % 2) * 64 + ((zz + NZ) % NZ) * cols
        return wg.at[pl.ds(pl.multiple_of(start, 16), cols)]

    def w_part(yy, zz, part):
        return w_slot(yy, zz).at[:, pl.ds(part * quarter, quarter)]

    def w_copy(yy, zz, part, peer, number, own=False):
        there = w_part(yy, zz, part)
        here = wt_hbm.at[:, pl.ds(part * quarter, quarter)] if own else there
        return pltpu.make_async_remote_copy(
            src_ref=here, dst_ref=there,
            send_sem=w_send.at[number], recv_sem=w_recv.at[yy % 2, (zz + NZ) % NZ, part],
            device_id={"seq": peer}, device_id_type=MESH,
        )

    def w_wait(yy, zz, part):
        w_copy(yy, zz, part, me, 0).wait_recv()

    local_copies = [
        pltpu.make_async_copy(head_of(hbm, me), slot(me), local_sem.at[n])
        for n, (hbm, slot) in enumerate(streams)
    ] + [
        pltpu.make_async_copy(wt_hbm, w_slot(y, z), local_sem.at[3]),
        pltpu.make_async_copy(res_hbm, res_s, local_sem.at[4]),
        pltpu.make_async_copy(mask_hbm, mask_s, local_sem.at[5]),
        pltpu.make_async_copy(gates_hbm, gates_s, local_sem.at[6]),
    ]
    for copy in local_copies:
        copy.start()

    barrier = pltpu.get_barrier_semaphore()

    @pl.loop(1, SEQ)
    def _(k):
        pl.semaphore_signal(
            barrier, inc=1, device_id={"seq": (me + k) % SEQ}, device_id_type=MESH
        )

    pl.semaphore_signal(barrier, inc=1, device_id={"branch": 1 - branch}, device_id_type=MESH)
    pl.semaphore_wait(barrier, SEQ)

    def peer_at(k):
        return index(y + k // PLANE, x + (k // NZ) % NX, z + k % NZ)

    def offset(step):
        left = 2 * NZ - 1 - step // 2
        return left // NZ, left % NZ

    for number in (1, 2):
        @pl.loop(1, SEQ)
        def _(k):
            qkv_copy(number, peer_at(k), me).start()

    def send_queries(k):
        dy, dz = offset(k // NX * 2)
        qkv_copy(0, index(y + dy, x + k % NX, z + NZ - dz), me).start()

    pl.loop(0, SEQ - NX)(send_queries)
    pl.loop(SEQ - NX + 1, SEQ)(send_queries)

    for at, part in enumerate((2, 3)):
        w_copy(y, z, part, index(y, x, z + 1), 2 * at, True).start()
        w_copy(y, z, part, index(y, x, z - 1), 2 * at + 1, True).start()
        w_copy(y, z, part - 2, index(y + 1, x, z), 4 + at, True).start()
    v_s[:, DH:] = jnp.ones((keys, DH), jnp.bfloat16)
    for yy in range(2):
        spare = pl.multiple_of(yy * wide + (1 - x % 2) * (wide - 64), 64)
        wg[pl.ds(spare, 64), :] = jnp.zeros((64, wg.shape[1]), jnp.bfloat16)

    def along_z(part, other):
        if other:
            w_wait(y + 1, z, part)
        for at, way in enumerate((1, -1)):
            number = 6 + 4 * part + 2 * other + at
            w_copy(y + other, z, part, index(y, x, z + way), number, not other).start()

    def over_y(part, step):
        if step:
            w_wait(y, z + step, part)
        number = 14 + 4 * (part - 2) + step % NZ
        w_copy(y, z + step, part, index(y + 1, x, z), number, step == 0).start()

    def relay_z(part):
        if part < 2:
            for yy, way in enumerate((1, -1)):
                w_wait(yy, z - way, part)
                w_copy(yy, z - way, part, index(y, x, z + way), 22 + 2 * part + yy).start()
        else:
            way = 1 if part == 2 else -1
            w_copy(y, z - way, part, index(y, x, z + way), 24 + part).start()

    actions = (
        lambda: along_z(0, 0),
        lambda: (along_z(0, 1), over_y(2, 0)),
        lambda: (along_z(1, 0), over_y(3, 0)),
        lambda: (over_y(2, -1), relay_z(2), over_y(3, 1), relay_z(3)),
        lambda: along_z(1, 1),
        lambda: (over_y(2, 1), over_y(3, -1)),
        lambda: relay_z(0),
        lambda: relay_z(1),
        lambda: over_y(2, 2),
        lambda: over_y(3, 2),
    )
    events = tuple(zip(W_STEPS, actions))

    def await_queries(step):
        dy, dz = offset(step)
        for tile in range(2):
            source = index(y + dy, 2 * (step % 2) + tile, z + dz)
            pl.when(source != me)(lambda source=source: qkv_copy(0, me, source).wait_recv())

    def attend(step, now, following):
        lanes = KEY_CHUNK // DH
        if following is not None:
            scores_ref, peak_ref = following
            await_queries(step + 1)
            dy, dz = offset(step + 1)
            place = (((y + dy) % 2) * NZ + (z + dz) % NZ) * 2 + (step + 1) % 2
            query = q_s[aligned(place, block), :]
            peak = None
        if now is not None:
            held_ref, held_peak = now
            total = jnp.zeros((block, 2 * DH), jnp.float32)
        for chunk in range(keys // KEY_CHUNK):
            span = pl.ds(chunk * KEY_CHUNK, KEY_CHUNK)
            if following is not None:
                scores = lax.dot_general(
                    query, k_s[span, :], NT, preferred_element_type=jnp.float32
                )
                scores_ref[:, span] = scores
                for lane in range(lanes):
                    piece = scores[:, lane * DH : (lane + 1) * DH]
                    peak = piece if peak is None else jnp.maximum(peak, piece)
            if now is not None:
                shift = held_peak[...]
                probs = [
                    jnp.exp2(
                        held_ref[:, pl.ds(chunk * KEY_CHUNK + lane * DH, DH)] * factor - shift
                    ).astype(jnp.bfloat16)
                    for lane in range(lanes)
                ]
                total += jnp.dot(
                    jnp.concatenate(probs, axis=1), v_s[span, :],
                    preferred_element_type=jnp.float32,
                )
        if following is not None:
            top = jnp.max(peak, axis=1, keepdims=True) * factor
            peak_ref[...] = jnp.broadcast_to(top, (block, DH))
        if now is not None:
            o_s[step] = (total[:, :DH] / total[:, DH:]).astype(jnp.bfloat16)

    def att_part(head, half):
        return att.at[aligned(half, block), aligned(head, DH)]

    def a_copy(head, half, peer, send_sem, source=None):
        part = att_part(head, half)
        return pltpu.make_async_remote_copy(
            src_ref=part if source is None else source, dst_ref=part,
            send_sem=send_sem, recv_sem=a_recv.at[head, half],
            device_id={"seq": peer}, device_id_type=MESH,
        )

    def a_wait(head, half):
        a_copy(head, half, me, a_send.at[0]).wait_recv()

    def deliver(step):
        dy, dz = offset(step)
        peer = index(y + dy, x, z + dz)
        a_copy(me, step % 2, peer, a_send.at[step], o_s.at[step]).start()

    def spread(step):
        dy, dz = offset(step)
        head = index(y + dy, x, z + NZ - dz)
        a_wait(head, step % 2)
        for at, way in enumerate((1, -1)):
            a_copy(head, step % 2, index(y, x + way, z), f_send.at[step, at]).start()

    def spread_own(step):
        for at, way in enumerate((1, -1)):
            a_copy(
                me, step % 2, index(y, x + way, z), f_send.at[step, at], o_s.at[step]
            ).start()

    def relay(step):
        dy, dz = offset(step)
        way = 1 - 2 * (step % 2)
        head = index(y + dy, x - way, z + NZ - dz)
        a_wait(head, step % 2)
        a_copy(head, step % 2, index(y, x + way, z), g_send.at[step]).start()

    first, second = (s_a, m_a), (s_b, m_b)
    local_copies[0].wait()
    for number in (1, 2):
        local_copies[number].wait()

        @pl.loop(1, SEQ)
        def _(k):
            qkv_copy(number, me, (me + k) % SEQ).wait_recv()

        if number == 1:
            attend(-1, None, first)

    @pl.loop(0, steps // 2 - 1)
    def _(pair):
        for part in range(2):
            step = pair * 2 + part
            for at, event in events:
                if at % 2 == part:
                    pl.when(pair == at // 2)(lambda event=event: event() and None)
            attend(step, (first, second)[part], (second, first)[part])
            deliver(step)

            @pl.when(step >= SPREAD_LAG)
            def _():
                spread(step - SPREAD_LAG)

            @pl.when(step >= RELAY_LAG)
            def _():
                relay(step - RELAY_LAG)

    own_parts = [
        pltpu.make_async_copy(
            o_s.at[steps - 2 + half], att_part(me, half), local_sem.at[7 + half]
        )
        for half in range(2)
    ]
    for half in range(2):
        step = steps - 2 + half
        attend(step, (first, second)[half], second if half == 0 else None)
        own_parts[half].start()
        spread_own(step)
        if step - SPREAD_LAG < steps - 2:
            spread(step - SPREAD_LAG)
        relay(step - RELAY_LAG)

    @pl.loop(steps - SPREAD_LAG, steps - 2)
    def _(step):
        spread(step)

    @pl.loop(steps - RELAY_LAG, steps)
    def _(step):
        relay(step)

    for copy in local_copies[3:] + own_parts:
        copy.wait()
    for part in range(2):
        for yy, way in enumerate((1, -1)):
            w_wait(yy, z + way, part)
            w_wait(yy, z + 2, part)
        for step in range(NZ):
            w_wait(y + 1, z + step, part + 2)

    @pl.loop(0, steps)
    def _(step):
        dy, dz = offset(step)
        way = 1 - 2 * (step % 2)
        a_wait(index(y + dy, x + way, z + NZ - dz), step % 2)
        a_wait(index(y + dy, x + 2, z + NZ - dz), step % 2)

    def r_copy(yy, tile, source):
        return pltpu.make_async_remote_copy(
            src_ref=sbuf.at[yy, aligned(tile, rows)], dst_ref=rbuf.at[source, yy],
            send_sem=r_send.at[yy, tile], recv_sem=r_recv.at[yy, source],
            device_id={"seq": index(y, tile, z)}, device_id_type=MESH,
        )

    half_width = out_ref.shape[1] // 2

    def h_copy(yy):
        span = pl.ds(yy * half_width, half_width)
        return pltpu.make_async_remote_copy(
            src_ref=out_ref.at[:, span], dst_ref=hints.at[yy],
            send_sem=h_send.at[yy], recv_sem=h_recv.at[yy],
            device_id={"branch": 1 - branch}, device_id_type=MESH,
        )

    for yy in range(2):
        sbuf[yy] = lax.dot_general(
            att[...], wg[pl.ds(yy * wide, wide), :], NT, preferred_element_type=jnp.float32
        ).astype(jnp.bfloat16)
        for step in (1, 3, 2):
            r_copy(yy, (x + step) % NX, x).start()

    chosen = mask_s[...] == 1
    gate = gates_s[pl.ds(index_ref[0], 1), :]
    low = lax.broadcasted_iota(jnp.int32, (rows, DH), 1) < DH // 2
    for yy in range(2):
        rbuf[x, yy] = sbuf[yy, aligned(x, rows), :]
        for step in (1, 3, 2):
            r_copy(yy, x, (x + step) % NX).wait_recv()
        tiles = []
        for pair in range(NX // 2):
            even = rbuf[2 * pair, yy].astype(jnp.float32)
            odd = rbuf[2 * pair + 1, yy].astype(jnp.float32)
            tiles += [
                even[:, : wide - DH], jnp.where(low, even[:, wide - DH :], odd[:, :DH]),
                odd[:, DH:],
            ]
        projected = jnp.concatenate(tiles, axis=1)
        span = pl.ds(yy * half_width, half_width)

        @pl.when(branch == 0)
        def _():
            out_ref[:, span] = jnp.where(chosen, projected, 0.0).astype(jnp.bfloat16)
            h_copy(yy).start()

        @pl.when(branch == 1)
        def _():
            h_copy(yy).wait_recv()
            out_ref[:, span] = (
                res_s[:, span].astype(jnp.float32)
                + gate[:, yy * half_width : (yy + 1) * half_width] * projected
                + hints[yy].astype(jnp.float32)
            ).astype(jnp.bfloat16)

    for number in range(3):
        @pl.loop(1, SEQ)
        def _(k):
            qkv_copy(number, (me + k) % SEQ, me).wait_send()

    for number in range(28):
        w_copy(0, 0, 0, me, number).wait_send()

    @pl.loop(0, steps - 2)
    def _(step):
        a_copy(0, 0, me, a_send.at[step]).wait_send()

    @pl.loop(0, steps)
    def _(step):
        for at in range(2):
            a_copy(0, 0, me, f_send.at[step, at]).wait_send()
        a_copy(0, 0, me, g_send.at[step]).wait_send()

    for yy in range(2):
        for step in (1, 3, 2):
            r_copy(yy, (x + step) % NX, x).wait_send()

        @pl.when(branch == 0)
        def _():
            h_copy(yy).wait_send()


def per_device(
    query_rows, key_rows, value_rows, residual, control_mask, step_index, step_gates, out_weight
):
    rows = query_rows.shape[1]
    tokens = rows * SEQ
    block = 2 * rows
    steps = tokens // block
    width = residual.shape[1]
    features = out_weight.shape[1]
    wide = NZ * out_weight.shape[2] + 64
    weight_rows = jnp.swapaxes(out_weight[0], 0, 1)
    bf16, f32 = jnp.bfloat16, jnp.float32
    hbm = pl.BlockSpec(memory_space=pl.ANY)
    dma = pltpu.SemaphoreType.DMA
    block_out = pl.pallas_call(
        fused_kernel,
        out_shape=jax.ShapeDtypeStruct((rows, width), bf16),
        in_specs=[pl.BlockSpec(memory_space=pltpu.SMEM)] + [hbm] * 7,
        out_specs=pl.BlockSpec(memory_space=pltpu.VMEM),
        scratch_shapes=[
            pltpu.VMEM((tokens, DH), bf16),
            pltpu.VMEM((tokens, DH), bf16),
            pltpu.VMEM((tokens, 2 * DH), bf16),
            pltpu.VMEM((block, tokens), f32),
            pltpu.VMEM((block, tokens), f32),
            pltpu.VMEM((block, DH), f32),
            pltpu.VMEM((block, DH), f32),
            pltpu.VMEM((steps, block, DH), bf16),
            pltpu.VMEM((NX * rows, features), bf16),
            pltpu.VMEM((2 * wide, features), bf16),
            pltpu.VMEM((2, NX * rows, wide), bf16),
            pltpu.VMEM((NX, 2, rows, wide), bf16),
            pltpu.VMEM((2, rows, width // 2), bf16),
            pltpu.VMEM((rows, width), bf16),
            pltpu.VMEM((rows, 1), jnp.int32),
            pltpu.VMEM(step_gates.shape, f32),
            dma((3, SEQ)), dma((3, SEQ)), dma((9,)), dma((28,)), dma((2, NZ, 4)),
            dma((steps,)), dma((SEQ, 2)), dma((steps, 2)), dma((steps,)),
            dma((2, NX)), dma((2, NX)), dma((2,)), dma((2,)),
        ],
        compiler_params=pltpu.CompilerParams(
            collective_id=0, has_side_effects=True, vmem_limit_bytes=60000 * 1024
        ),
        name="attend_project",
    )(
        step_index, query_rows, key_rows, value_rows, weight_rows, residual,
        control_mask[:, None], step_gates,
    )
    return block_out[None]


def solution(mesh):
    placed = (
        P("branch", ("group", "seq"), None),
        P("branch", ("group", "seq"), None),
        P("branch", ("group", "seq"), None),
        P(("group", "seq"), None),
        P(("group", "seq")),
        P("group"),
        P(),
        P("branch", None, "seq"),
    )
    return jax.shard_map(
        per_device,
        mesh=mesh,
        in_specs=placed,
        out_specs=P("branch", ("group", "seq"), None),
        check_vma=False,
    )
```

```python
import math

import jax
import jax.numpy as jnp
from jax import lax
from jax.experimental import pallas as pl
from jax.experimental.pallas import tpu as pltpu
from jax.sharding import PartitionSpec as P

DH = 128
NX = 4
NZ = 4
PLANE = NX * NZ
SEQ = 2 * PLANE
MESH = pl.DeviceIdType.MESH
KEY_CHUNK = 512
OUT_CHUNK = 256
SPREAD_LAG = 2
RELAY_LAG = 4
W_STEPS = (5, 6, 7, 8, 9, 10, 11, 12, 12, 13)
NT = (((1,), (1,)), ((), ()))


def fused_kernel(
    index_ref, q_hbm, k_hbm, v_hbm, wt_hbm, res_hbm, mask_hbm, gates_hbm, out_ref,
    q_s, k_s, v_s, s_a, s_b, m_a, m_b, o_s, att, wg, sbuf, rbuf, hints, res_s, mask_s, gates_s,
    qkv_send, qkv_recv, local_sem, w_send, w_recv, a_send, a_recv, f_send, g_send,
    r_send, r_recv, h_send, h_recv,
):
    rows = q_hbm.shape[1]
    cols = wt_hbm.shape[0]
    keys = k_s.shape[0]
    block = 2 * rows
    steps = keys // block
    wide = rbuf.shape[2] // 2
    quarter = wt_hbm.shape[1] // 4
    factor = float(DH) ** -0.5 * math.log2(math.e)
    branch = lax.axis_index("branch")
    me = lax.axis_index("seq")
    y = me // PLANE
    x = (me // NZ) % NX
    z = me % NZ

    def index(yy, xx, zz):
        return (yy % 2) * PLANE + ((xx + NX) % NX) * NZ + (zz + NZ) % NZ

    def aligned(value, step):
        return pl.ds(pl.multiple_of(value * step, step), step)

    def q_slot(source):
        order = ((source // PLANE) * NZ + source % NZ) * NX + (source // NZ) % NX
        return q_s.at[aligned(order, rows)]

    def k_slot(source):
        return k_s.at[aligned(source, rows)]

    def v_slot(source):
        return v_s.at[aligned(source, rows), pl.ds(0, DH)]

    streams = ((q_hbm, q_slot), (k_hbm, k_slot), (v_hbm, v_slot))

    def head_of(hbm, head):
        return hbm.at[0, :, aligned(head, DH)]

    def qkv_copy(number, peer, source):
        hbm, slot = streams[number]
        return pltpu.make_async_remote_copy(
            src_ref=head_of(hbm, peer), dst_ref=slot(source),
            send_sem=qkv_send.at[number, peer], recv_sem=qkv_recv.at[number, source],
            device_id={"seq": peer}, device_id_type=MESH,
        )

    def w_slot(yy, zz):
        start = (yy % 2) * wide + (x % 2) * 64 + ((zz + NZ) % NZ) * cols
        return wg.at[pl.ds(pl.multiple_of(start, 16), cols)]

    def w_part(yy, zz, part):
        return w_slot(yy, zz).at[:, pl.ds(part * quarter, quarter)]

    def w_copy(yy, zz, part, peer, number, own=False):
        there = w_part(yy, zz, part)
        here = wt_hbm.at[:, pl.ds(part * quarter, quarter)] if own else there
        return pltpu.make_async_remote_copy(
            src_ref=here, dst_ref=there,
            send_sem=w_send.at[number], recv_sem=w_recv.at[yy % 2, (zz + NZ) % NZ, part],
            device_id={"seq": peer}, device_id_type=MESH,
        )

    def w_wait(yy, zz, part):
        w_copy(yy, zz, part, me, 0).wait_recv()

    local_copies = [
        pltpu.make_async_copy(head_of(hbm, me), slot(me), local_sem.at[n])
        for n, (hbm, slot) in enumerate(streams)
    ] + [
        pltpu.make_async_copy(wt_hbm, w_slot(y, z), local_sem.at[3]),
        pltpu.make_async_copy(res_hbm, res_s, local_sem.at[4]),
        pltpu.make_async_copy(mask_hbm, mask_s, local_sem.at[5]),
        pltpu.make_async_copy(gates_hbm, gates_s, local_sem.at[6]),
    ]
    for copy in local_copies:
        copy.start()

    barrier = pltpu.get_barrier_semaphore()

    @pl.loop(1, SEQ)
    def _(k):
        pl.semaphore_signal(
            barrier, inc=1, device_id={"seq": (me + k) % SEQ}, device_id_type=MESH
        )

    pl.semaphore_signal(barrier, inc=1, device_id={"branch": 1 - branch}, device_id_type=MESH)
    pl.semaphore_wait(barrier, SEQ)

    def peer_at(k):
        return index(y + k // PLANE, x + (k // NZ) % NX, z + k % NZ)

    def offset(step):
        left = 2 * NZ - 1 - step // 2
        return left // NZ, left % NZ

    for number in (1, 2):
        @pl.loop(1, SEQ)
        def _(k):
            qkv_copy(number, peer_at(k), me).start()

    def send_queries(k):
        dy, dz = offset(k // NX * 2)
        qkv_copy(0, index(y + dy, x + k % NX, z + NZ - dz), me).start()

    pl.loop(0, SEQ - NX)(send_queries)
    pl.loop(SEQ - NX + 1, SEQ)(send_queries)

    for at, part in enumerate((2, 3)):
        w_copy(y, z, part, index(y, x, z + 1), 2 * at, True).start()
        w_copy(y, z, part, index(y, x, z - 1), 2 * at + 1, True).start()
        w_copy(y, z, part - 2, index(y + 1, x, z), 4 + at, True).start()
    v_s[:, DH:] = jnp.ones((keys, DH), jnp.bfloat16)
    for yy in range(2):
        spare = pl.multiple_of(yy * wide + (1 - x % 2) * (wide - 64), 64)
        wg[pl.ds(spare, 64), :] = jnp.zeros((64, wg.shape[1]), jnp.bfloat16)

    def along_z(part, other):
        if other:
            w_wait(y + 1, z, part)
        for at, way in enumerate((1, -1)):
            number = 6 + 4 * part + 2 * other + at
            w_copy(y + other, z, part, index(y, x, z + way), number, not other).start()

    def over_y(part, step):
        if step:
            w_wait(y, z + step, part)
        number = 14 + 4 * (part - 2) + step % NZ
        w_copy(y, z + step, part, index(y + 1, x, z), number, step == 0).start()

    def relay_z(part):
        if part < 2:
            for yy, way in enumerate((1, -1)):
                w_wait(yy, z - way, part)
                w_copy(yy, z - way, part, index(y, x, z + way), 22 + 2 * part + yy).start()
        else:
            way = 1 if part == 2 else -1
            w_copy(y, z - way, part, index(y, x, z + way), 24 + part).start()

    actions = (
        lambda: along_z(0, 0),
        lambda: (along_z(0, 1), over_y(2, 0)),
        lambda: (along_z(1, 0), over_y(3, 0)),
        lambda: (over_y(2, -1), relay_z(2), over_y(3, 1), relay_z(3)),
        lambda: along_z(1, 1),
        lambda: (over_y(2, 1), over_y(3, -1)),
        lambda: relay_z(0),
        lambda: relay_z(1),
        lambda: over_y(2, 2),
        lambda: over_y(3, 2),
    )
    events = tuple(zip(W_STEPS, actions))

    def await_queries(step):
        dy, dz = offset(step)
        for tile in range(2):
            source = index(y + dy, 2 * (step % 2) + tile, z + dz)
            pl.when(source != me)(lambda source=source: qkv_copy(0, me, source).wait_recv())

    def attend(step, now, following):
        lanes = KEY_CHUNK // DH
        if following is not None:
            scores_ref, peak_ref = following
            await_queries(step + 1)
            dy, dz = offset(step + 1)
            place = (((y + dy) % 2) * NZ + (z + dz) % NZ) * 2 + (step + 1) % 2
            query = q_s[aligned(place, block), :]
            peak = None
        if now is not None:
            held_ref, held_peak = now
            total = jnp.zeros((block, 2 * DH), jnp.float32)
        for chunk in range(keys // KEY_CHUNK):
            span = pl.ds(chunk * KEY_CHUNK, KEY_CHUNK)
            if following is not None:
                scores = lax.dot_general(
                    query, k_s[span, :], NT, preferred_element_type=jnp.float32
                )
                scores_ref[:, span] = scores
                for lane in range(lanes):
                    piece = scores[:, lane * DH : (lane + 1) * DH]
                    peak = piece if peak is None else jnp.maximum(peak, piece)
            if now is not None:
                shift = held_peak[...]
                probs = [
                    jnp.exp2(
                        held_ref[:, pl.ds(chunk * KEY_CHUNK + lane * DH, DH)] * factor - shift
                    ).astype(jnp.bfloat16)
                    for lane in range(lanes)
                ]
                total += jnp.dot(
                    jnp.concatenate(probs, axis=1), v_s[span, :],
                    preferred_element_type=jnp.float32,
                )
        if following is not None:
            top = jnp.max(peak, axis=1, keepdims=True) * factor
            peak_ref[...] = jnp.broadcast_to(top, (block, DH))
        if now is not None:
            o_s[step] = (total[:, :DH] / total[:, DH:]).astype(jnp.bfloat16)

    def att_part(head, half):
        return att.at[aligned(half, block), aligned(head, DH)]

    def a_copy(head, half, peer, send_sem, source=None):
        part = att_part(head, half)
        return pltpu.make_async_remote_copy(
            src_ref=part if source is None else source, dst_ref=part,
            send_sem=send_sem, recv_sem=a_recv.at[head, half],
            device_id={"seq": peer}, device_id_type=MESH,
        )

    def a_wait(head, half):
        a_copy(head, half, me, a_send.at[0]).wait_recv()

    def deliver(step):
        dy, dz = offset(step)
        peer = index(y + dy, x, z + dz)
        a_copy(me, step % 2, peer, a_send.at[step], o_s.at[step]).start()

    def spread(step):
        dy, dz = offset(step)
        head = index(y + dy, x, z + NZ - dz)
        a_wait(head, step % 2)
        for at, way in enumerate((1, -1)):
            a_copy(head, step % 2, index(y, x + way, z), f_send.at[step, at]).start()

    def spread_own(step):
        for at, way in enumerate((1, -1)):
            a_copy(
                me, step % 2, index(y, x + way, z), f_send.at[step, at], o_s.at[step]
            ).start()

    def relay(step):
        dy, dz = offset(step)
        way = 1 - 2 * (step % 2)
        head = index(y + dy, x - way, z + NZ - dz)
        a_wait(head, step % 2)
        a_copy(head, step % 2, index(y, x + way, z), g_send.at[step]).start()

    first, second = (s_a, m_a), (s_b, m_b)
    local_copies[0].wait()
    for number in (1, 2):
        local_copies[number].wait()

        @pl.loop(1, SEQ)
        def _(k):
            qkv_copy(number, me, (me + k) % SEQ).wait_recv()

        if number == 1:
            attend(-1, None, first)

    @pl.loop(0, steps // 2 - 1)
    def _(pair):
        for part in range(2):
            step = pair * 2 + part
            for at, event in events:
                if at % 2 == part:
                    pl.when(pair == at // 2)(lambda event=event: event() and None)
            attend(step, (first, second)[part], (second, first)[part])
            deliver(step)

            @pl.when(step >= SPREAD_LAG)
            def _():
                spread(step - SPREAD_LAG)

            @pl.when(step >= RELAY_LAG)
            def _():
                relay(step - RELAY_LAG)

    own_parts = [
        pltpu.make_async_copy(
            o_s.at[steps - 2 + half], att_part(me, half), local_sem.at[7 + half]
        )
        for half in range(2)
    ]
    for half in range(2):
        step = steps - 2 + half
        attend(step, (first, second)[half], second if half == 0 else None)
        own_parts[half].start()
        spread_own(step)
        if step - SPREAD_LAG < steps - 2:
            spread(step - SPREAD_LAG)
        relay(step - RELAY_LAG)

    @pl.loop(steps - SPREAD_LAG, steps - 2)
    def _(step):
        spread(step)

    @pl.loop(steps - RELAY_LAG, steps)
    def _(step):
        relay(step)

    for copy in local_copies[3:] + own_parts:
        copy.wait()

    for part in range(2):
        for yy, way in enumerate((1, -1)):
            w_wait(yy, z + way, part)
            w_wait(yy, z + 2, part)
        for step in range(NZ):
            w_wait(y + 1, z + step, part + 2)

    @pl.loop(0, steps)
    def _(step):
        dy, dz = offset(step)
        way = 1 - 2 * (step % 2)
        a_wait(index(y + dy, x + way, z + NZ - dz), step % 2)
        a_wait(index(y + dy, x + 2, z + NZ - dz), step % 2)

    def part_of(chunk):
        return pl.ds(chunk * OUT_CHUNK, OUT_CHUNK)

    def r_copy(chunk, tile, source):
        return pltpu.make_async_remote_copy(
            src_ref=sbuf.at[aligned(tile, rows), part_of(chunk)],
            dst_ref=rbuf.at[source, :, part_of(chunk)],
            send_sem=r_send.at[chunk, tile], recv_sem=r_recv.at[chunk, source],
            device_id={"seq": index(y, tile, z)}, device_id_type=MESH,
        )

    chunks = 2 * wide // OUT_CHUNK
    piece_width = out_ref.shape[1] // 4

    def h_copy(piece):
        return pltpu.make_async_remote_copy(
            src_ref=out_ref.at[:, pl.ds(piece * piece_width, piece_width)],
            dst_ref=hints.at[piece],
            send_sem=h_send.at[piece], recv_sem=h_recv.at[piece],
            device_id={"branch": 1 - branch}, device_id_type=MESH,
        )

    for chunk in range(chunks):
        sbuf[:, part_of(chunk)] = lax.dot_general(
            att[...], wg[part_of(chunk), :], NT, preferred_element_type=jnp.float32
        ).astype(jnp.bfloat16)
        for step in (1, 3, 2):
            r_copy(chunk, (x + step) % NX, x).start()

    chosen = mask_s[...] == 1
    gate = gates_s[pl.ds(index_ref[0], 1), :]
    rbuf[x] = sbuf[aligned(x, rows), :]
    low = lax.broadcasted_iota(jnp.int32, (rows, DH), 1) < DH // 2
    for yy in range(2):
        for chunk in (range(2), range(2, chunks))[yy]:
            for step in (1, 3, 2):
                r_copy(chunk, x, (x + step) % NX).wait_recv()
        for pair in range(2):
            even = rbuf[2 * pair, :, pl.ds(yy * wide, wide)].astype(jnp.float32)
            odd = rbuf[2 * pair + 1, :, pl.ds(yy * wide, wide)].astype(jnp.float32)
            projected = jnp.concatenate(
                [
                    even[:, : wide - DH], jnp.where(low, even[:, wide - DH :], odd[:, :DH]),
                    odd[:, DH:],
                ],
                axis=1,
            )
            piece = 2 * yy + pair
            start = piece * piece_width
            span = pl.ds(start, piece_width)

            @pl.when(branch == 0)
            def _():
                out_ref[:, span] = jnp.where(chosen, projected, 0.0).astype(jnp.bfloat16)
                h_copy(piece).start()

            @pl.when(branch == 1)
            def _():
                h_copy(piece).wait_recv()
                out_ref[:, span] = (
                    res_s[:, span].astype(jnp.float32)
                    + gate[:, start : start + piece_width] * projected
                    + hints[piece].astype(jnp.float32)
                ).astype(jnp.bfloat16)

    for number in range(3):
        @pl.loop(1, SEQ)
        def _(k):
            qkv_copy(number, (me + k) % SEQ, me).wait_send()

    for chunk in range(chunks):
        for step in (1, 3, 2):
            r_copy(chunk, (x + step) % NX, x).wait_send()

    for number in range(28):
        w_copy(0, 0, 0, me, number).wait_send()

    @pl.loop(0, steps - 2)
    def _(step):
        a_copy(0, 0, me, a_send.at[step]).wait_send()

    @pl.loop(0, steps)
    def _(step):
        for at in range(2):
            a_copy(0, 0, me, f_send.at[step, at]).wait_send()
        a_copy(0, 0, me, g_send.at[step]).wait_send()

    for yy in range(2):
        @pl.when(branch == 0)
        def _():
            for pair in range(2):
                h_copy(2 * yy + pair).wait_send()


def per_device(
    query_rows, key_rows, value_rows, residual, control_mask, step_index, step_gates, out_weight
):
    rows = query_rows.shape[1]
    tokens = rows * SEQ
    block = 2 * rows
    steps = tokens // block
    width = residual.shape[1]
    features = out_weight.shape[1]
    wide = NZ * out_weight.shape[2] + 64
    weight_rows = jnp.swapaxes(out_weight[0], 0, 1)
    bf16, f32 = jnp.bfloat16, jnp.float32
    hbm = pl.BlockSpec(memory_space=pl.ANY)
    dma = pltpu.SemaphoreType.DMA
    block_out = pl.pallas_call(
        fused_kernel,
        out_shape=jax.ShapeDtypeStruct((rows, width), bf16),
        in_specs=[pl.BlockSpec(memory_space=pltpu.SMEM)] + [hbm] * 7,
        out_specs=pl.BlockSpec(memory_space=pltpu.VMEM),
        scratch_shapes=[
            pltpu.VMEM((tokens, DH), bf16),
            pltpu.VMEM((tokens, DH), bf16),
            pltpu.VMEM((tokens, 2 * DH), bf16),
            pltpu.VMEM((block, tokens), f32),
            pltpu.VMEM((block, tokens), f32),
            pltpu.VMEM((block, DH), f32),
            pltpu.VMEM((block, DH), f32),
            pltpu.VMEM((steps, block, DH), bf16),
            pltpu.VMEM((NX * rows, features), bf16),
            pltpu.VMEM((2 * wide, features), bf16),
            pltpu.VMEM((NX * rows, 2 * wide), bf16),
            pltpu.VMEM((NX, rows, 2 * wide), bf16),
            pltpu.VMEM((4, rows, width // 4), bf16),
            pltpu.VMEM((rows, width), bf16),
            pltpu.VMEM((rows, 1), jnp.int32),
            pltpu.VMEM(step_gates.shape, f32),
            dma((3, SEQ)), dma((3, SEQ)), dma((9,)), dma((28,)), dma((2, NZ, 4)),
            dma((steps,)), dma((SEQ, 2)), dma((steps, 2)), dma((steps,)),
            dma((3, NX)), dma((3, NX)), dma((4,)), dma((4,)),
        ],
        compiler_params=pltpu.CompilerParams(
            collective_id=0, has_side_effects=True, vmem_limit_bytes=60000 * 1024
        ),
        name="attend_project",
    )(
        step_index, query_rows, key_rows, value_rows, weight_rows, residual,
        control_mask[:, None], step_gates,
    )
    return block_out[None]


def solution(mesh):
    placed = (
        P("branch", ("group", "seq"), None),
        P("branch", ("group", "seq"), None),
        P("branch", ("group", "seq"), None),
        P(("group", "seq"), None),
        P(("group", "seq")),
        P("group"),
        P(),
        P("branch", None, "seq"),
    )
    return jax.shard_map(
        per_device,
        mesh=mesh,
        in_specs=placed,
        out_specs=P("branch", ("group", "seq"), None),
        check_vma=False,
    )
```

```python
import math

import jax
import jax.numpy as jnp
from jax import lax
from jax.experimental import pallas as pl
from jax.experimental.pallas import tpu as pltpu
from jax.sharding import PartitionSpec as P

DH = 128
NX = 4
NZ = 4
PLANE = NX * NZ
SEQ = 2 * PLANE
MESH = pl.DeviceIdType.MESH
KEY_CHUNK = 512
OUT_CHUNK = 256
SPREAD_LAG = 2
RELAY_LAG = 4
W_STEPS = (5, 6, 7, 8, 9, 10, 11, 12, 12, 13)
NT = (((1,), (1,)), ((), ()))


def fused_kernel(
    index_ref, q_hbm, k_hbm, v_hbm, wt_hbm, res_hbm, mask_hbm, gates_hbm, out_ref,
    q_s, k_s, v_s, s_a, s_b, m_a, m_b, o_s, att, wg, sbuf, rbuf, hints, res_s, mask_s, gates_s,
    qkv_send, qkv_recv, local_sem, w_send, w_recv, a_send, a_recv, f_send, g_send,
    r_send, r_recv, h_send, h_recv,
):
    rows = q_hbm.shape[1]
    cols = wt_hbm.shape[0]
    keys = k_s.shape[0]
    block = 2 * rows
    steps = keys // block
    wide = rbuf.shape[2] // 2
    quarter = wt_hbm.shape[1] // 4
    factor = float(DH) ** -0.5 * math.log2(math.e)
    branch = lax.axis_index("branch")
    me = lax.axis_index("seq")
    y = me // PLANE
    x = (me // NZ) % NX
    z = me % NZ

    def index(yy, xx, zz):
        return (yy % 2) * PLANE + ((xx + NX) % NX) * NZ + (zz + NZ) % NZ

    def aligned(value, step):
        return pl.ds(pl.multiple_of(value * step, step), step)

    def q_slot(source):
        order = ((source // PLANE) * NZ + source % NZ) * NX + (source // NZ) % NX
        return q_s.at[aligned(order, rows)]

    def k_slot(source):
        return k_s.at[aligned(source, rows)]

    def v_slot(source):
        return v_s.at[aligned(source, rows), pl.ds(0, DH)]

    streams = ((q_hbm, q_slot), (k_hbm, k_slot), (v_hbm, v_slot))

    def head_of(hbm, head):
        return hbm.at[0, :, aligned(head, DH)]

    def qkv_copy(number, peer, source):
        hbm, slot = streams[number]
        return pltpu.make_async_remote_copy(
            src_ref=head_of(hbm, peer), dst_ref=slot(source),
            send_sem=qkv_send.at[number, peer], recv_sem=qkv_recv.at[number, source],
            device_id={"seq": peer}, device_id_type=MESH,
        )

    def w_slot(yy, zz):
        start = (yy % 2) * wide + (x % 2) * 64 + ((zz + NZ) % NZ) * cols
        return wg.at[pl.ds(pl.multiple_of(start, 16), cols)]

    def w_part(yy, zz, part):
        return w_slot(yy, zz).at[:, pl.ds(part * quarter, quarter)]

    def w_copy(yy, zz, part, peer, number, own=False):
        there = w_part(yy, zz, part)
        here = wt_hbm.at[:, pl.ds(part * quarter, quarter)] if own else there
        return pltpu.make_async_remote_copy(
            src_ref=here, dst_ref=there,
            send_sem=w_send.at[number], recv_sem=w_recv.at[yy % 2, (zz + NZ) % NZ, part],
            device_id={"seq": peer}, device_id_type=MESH,
        )

    def w_wait(yy, zz, part):
        w_copy(yy, zz, part, me, 0).wait_recv()

    local_copies = [
        pltpu.make_async_copy(head_of(hbm, me), slot(me), local_sem.at[n])
        for n, (hbm, slot) in enumerate(streams)
    ] + [
        pltpu.make_async_copy(wt_hbm, w_slot(y, z), local_sem.at[3]),
        pltpu.make_async_copy(res_hbm, res_s, local_sem.at[4]),
        pltpu.make_async_copy(mask_hbm, mask_s, local_sem.at[5]),
        pltpu.make_async_copy(gates_hbm, gates_s, local_sem.at[6]),
    ]
    for copy in local_copies:
        copy.start()

    barrier = pltpu.get_barrier_semaphore()

    @pl.loop(1, SEQ)
    def _(k):
        pl.semaphore_signal(
            barrier, inc=1, device_id={"seq": (me + k) % SEQ}, device_id_type=MESH
        )

    pl.semaphore_signal(barrier, inc=1, device_id={"branch": 1 - branch}, device_id_type=MESH)
    pl.semaphore_wait(barrier, SEQ)

    def peer_at(k):
        return index(y + k // PLANE, x + (k // NZ) % NX, z + k % NZ)

    def offset(step):
        left = 2 * NZ - 1 - step // 2
        return left // NZ, left % NZ

    for number in (1, 2):
        @pl.loop(1, SEQ)
        def _(k):
            qkv_copy(number, peer_at(k), me).start()

    def send_queries(k):
        dy, dz = offset(k // NX * 2)
        qkv_copy(0, index(y + dy, x + k % NX, z + NZ - dz), me).start()

    pl.loop(0, SEQ - NX)(send_queries)
    pl.loop(SEQ - NX + 1, SEQ)(send_queries)

    for at, part in enumerate((2, 3)):
        w_copy(y, z, part, index(y, x, z + 1), 2 * at, True).start()
        w_copy(y, z, part, index(y, x, z - 1), 2 * at + 1, True).start()
        w_copy(y, z, part - 2, index(y + 1, x, z), 4 + at, True).start()
    v_s[:, DH:] = jnp.ones((keys, DH), jnp.bfloat16)
    for yy in range(2):
        spare = pl.multiple_of(yy * wide + (1 - x % 2) * (wide - 64), 64)
        wg[pl.ds(spare, 64), :] = jnp.zeros((64, wg.shape[1]), jnp.bfloat16)

    def along_z(part, other):
        if other:
            w_wait(y + 1, z, part)
        for at, way in enumerate((1, -1)):
            number = 6 + 4 * part + 2 * other + at
            w_copy(y + other, z, part, index(y, x, z + way), number, not other).start()

    def over_y(part, step):
        if step:
            w_wait(y, z + step, part)
        number = 14 + 4 * (part - 2) + step % NZ
        w_copy(y, z + step, part, index(y + 1, x, z), number, step == 0).start()

    def relay_z(part):
        if part < 2:
            for yy, way in enumerate((1, -1)):
                w_wait(yy, z - way, part)
                w_copy(yy, z - way, part, index(y, x, z + way), 22 + 2 * part + yy).start()
        else:
            way = 1 if part == 2 else -1
            w_copy(y, z - way, part, index(y, x, z + way), 24 + part).start()

    actions = (
        lambda: along_z(0, 0),
        lambda: (along_z(0, 1), over_y(2, 0)),
        lambda: (along_z(1, 0), over_y(3, 0)),
        lambda: (over_y(2, -1), relay_z(2), over_y(3, 1), relay_z(3)),
        lambda: along_z(1, 1),
        lambda: (over_y(2, 1), over_y(3, -1)),
        lambda: relay_z(0),
        lambda: relay_z(1),
        lambda: over_y(2, 2),
        lambda: over_y(3, 2),
    )
    events = tuple(zip(W_STEPS, actions))

    def await_queries(step):
        dy, dz = offset(step)
        for tile in range(2):
            source = index(y + dy, 2 * (step % 2) + tile, z + dz)
            pl.when(source != me)(lambda source=source: qkv_copy(0, me, source).wait_recv())

    def attend(step, now, following):
        lanes = KEY_CHUNK // DH
        if following is not None:
            scores_ref, peak_ref = following
            await_queries(step + 1)
            dy, dz = offset(step + 1)
            place = (((y + dy) % 2) * NZ + (z + dz) % NZ) * 2 + (step + 1) % 2
            query = q_s[aligned(place, block), :]
            peak = None
        if now is not None:
            held_ref, held_peak = now
            total = jnp.zeros((block, 2 * DH), jnp.float32)
        for chunk in range(keys // KEY_CHUNK):
            span = pl.ds(chunk * KEY_CHUNK, KEY_CHUNK)
            if following is not None:
                scores = lax.dot_general(
                    query, k_s[span, :], NT, preferred_element_type=jnp.float32
                )
                scores_ref[:, span] = scores
                for lane in range(lanes):
                    piece = scores[:, lane * DH : (lane + 1) * DH]
                    peak = piece if peak is None else jnp.maximum(peak, piece)
            if now is not None:
                shift = held_peak[...]
                probs = [
                    jnp.exp2(
                        held_ref[:, pl.ds(chunk * KEY_CHUNK + lane * DH, DH)] * factor - shift
                    ).astype(jnp.bfloat16)
                    for lane in range(lanes)
                ]
                total += jnp.dot(
                    jnp.concatenate(probs, axis=1), v_s[span, :],
                    preferred_element_type=jnp.float32,
                )
        if following is not None:
            top = jnp.max(peak, axis=1, keepdims=True) * factor
            peak_ref[...] = jnp.broadcast_to(top, (block, DH))
        if now is not None:
            o_s[step] = (total[:, :DH] / total[:, DH:]).astype(jnp.bfloat16)

    def att_part(head, half):
        return att.at[aligned(half, block), aligned(head, DH)]

    def a_copy(head, half, peer, send_sem, source=None):
        part = att_part(head, half)
        return pltpu.make_async_remote_copy(
            src_ref=part if source is None else source, dst_ref=part,
            send_sem=send_sem, recv_sem=a_recv.at[head, half],
            device_id={"seq": peer}, device_id_type=MESH,
        )

    def a_wait(head, half):
        a_copy(head, half, me, a_send.at[0]).wait_recv()

    def deliver(step):
        dy, dz = offset(step)
        peer = index(y + dy, x, z + dz)
        a_copy(me, step % 2, peer, a_send.at[step], o_s.at[step]).start()

    def spread(step):
        dy, dz = offset(step)
        head = index(y + dy, x, z + NZ - dz)
        a_wait(head, step % 2)
        for at, way in enumerate((1, -1)):
            a_copy(head, step % 2, index(y, x + way, z), f_send.at[step, at]).start()

    def spread_own(step):
        for at, way in enumerate((1, -1)):
            a_copy(
                me, step % 2, index(y, x + way, z), f_send.at[step, at], o_s.at[step]
            ).start()

    def relay(step):
        dy, dz = offset(step)
        way = 1 - 2 * (step % 2)
        head = index(y + dy, x - way, z + NZ - dz)
        a_wait(head, step % 2)
        a_copy(head, step % 2, index(y, x + way, z), g_send.at[step]).start()

    first, second = (s_a, m_a), (s_b, m_b)
    local_copies[0].wait()
    for number in (1, 2):
        local_copies[number].wait()

        @pl.loop(1, SEQ)
        def _(k):
            qkv_copy(number, me, (me + k) % SEQ).wait_recv()

        if number == 1:
            attend(-1, None, first)

    @pl.loop(0, steps // 2 - 1)
    def _(pair):
        for part in range(2):
            step = pair * 2 + part
            for at, event in events:
                if at % 2 == part:
                    pl.when(pair == at // 2)(lambda event=event: event() and None)
            attend(step, (first, second)[part], (second, first)[part])
            deliver(step)

            @pl.when(step >= SPREAD_LAG)
            def _():
                spread(step - SPREAD_LAG)

            @pl.when(step >= RELAY_LAG)
            def _():
                relay(step - RELAY_LAG)

    own_parts = [
        pltpu.make_async_copy(
            o_s.at[steps - 2 + half], att_part(me, half), local_sem.at[7 + half]
        )
        for half in range(2)
    ]
    for half in range(2):
        step = steps - 2 + half
        attend(step, (first, second)[half], second if half == 0 else None)
        own_parts[half].start()
        spread_own(step)
        if step - SPREAD_LAG < steps - 2:
            spread(step - SPREAD_LAG)
        relay(step - RELAY_LAG)

    @pl.loop(steps - SPREAD_LAG, steps - 2)
    def _(step):
        spread(step)

    @pl.loop(steps - RELAY_LAG, steps)
    def _(step):
        relay(step)

    for copy in local_copies[3:] + own_parts:
        copy.wait()

    for part in range(2):
        for yy, way in enumerate((1, -1)):
            w_wait(yy, z + way, part)
            w_wait(yy, z + 2, part)
        for step in range(NZ):
            w_wait(y + 1, z + step, part + 2)

    @pl.loop(0, steps)
    def _(step):
        dy, dz = offset(step)
        way = 1 - 2 * (step % 2)
        a_wait(index(y + dy, x + way, z + NZ - dz), step % 2)
        a_wait(index(y + dy, x + 2, z + NZ - dz), step % 2)

    def part_of(chunk):
        return pl.ds(chunk * OUT_CHUNK, OUT_CHUNK)

    def r_copy(chunk, tile, source):
        return pltpu.make_async_remote_copy(
            src_ref=sbuf.at[aligned(tile, rows), part_of(chunk)],
            dst_ref=rbuf.at[source, :, part_of(chunk)],
            send_sem=r_send.at[chunk, tile], recv_sem=r_recv.at[chunk, source],
            device_id={"seq": index(y, tile, z)}, device_id_type=MESH,
        )

    chunks = 2 * wide // OUT_CHUNK
    piece_width = out_ref.shape[1] // 4

    def h_copy(piece):
        return pltpu.make_async_remote_copy(
            src_ref=out_ref.at[:, pl.ds(piece * piece_width, piece_width)],
            dst_ref=hints.at[piece],
            send_sem=h_send.at[piece], recv_sem=h_recv.at[piece],
            device_id={"branch": 1 - branch}, device_id_type=MESH,
        )

    for chunk in range(chunks):
        sbuf[:, part_of(chunk)] = lax.dot_general(
            att[...], wg[part_of(chunk), :], NT, preferred_element_type=jnp.float32
        ).astype(jnp.bfloat16)
        for step in (2, 1, 3):
            r_copy(chunk, (x + step) % NX, x).start()

    chosen = mask_s[...] == 1
    gate = gates_s[pl.ds(index_ref[0], 1), :]
    rbuf[x] = sbuf[aligned(x, rows), :]
    low = lax.broadcasted_iota(jnp.int32, (rows, DH), 1) < DH // 2
    for yy in range(2):
        for chunk in (range(2), range(2, chunks))[yy]:
            for step in (2, 1, 3):
                r_copy(chunk, x, (x + step) % NX).wait_recv()
        for pair in range(2):
            even = rbuf[2 * pair, :, pl.ds(yy * wide, wide)].astype(jnp.float32)
            odd = rbuf[2 * pair + 1, :, pl.ds(yy * wide, wide)].astype(jnp.float32)
            projected = jnp.concatenate(
                [
                    even[:, : wide - DH], jnp.where(low, even[:, wide - DH :], odd[:, :DH]),
                    odd[:, DH:],
                ],
                axis=1,
            )
            piece = 2 * yy + pair
            start = piece * piece_width
            span = pl.ds(start, piece_width)

            @pl.when(branch == 0)
            def _():
                out_ref[:, span] = jnp.where(chosen, projected, 0.0).astype(jnp.bfloat16)
                h_copy(piece).start()

            @pl.when(branch == 1)
            def _():
                h_copy(piece).wait_recv()
                out_ref[:, span] = (
                    res_s[:, span].astype(jnp.float32)
                    + gate[:, start : start + piece_width] * projected
                    + hints[piece].astype(jnp.float32)
                ).astype(jnp.bfloat16)

    for number in range(3):
        @pl.loop(1, SEQ)
        def _(k):
            qkv_copy(number, (me + k) % SEQ, me).wait_send()

    for chunk in range(chunks):
        for step in (2, 1, 3):
            r_copy(chunk, (x + step) % NX, x).wait_send()

    for number in range(28):
        w_copy(0, 0, 0, me, number).wait_send()

    @pl.loop(0, steps - 2)
    def _(step):
        a_copy(0, 0, me, a_send.at[step]).wait_send()

    @pl.loop(0, steps)
    def _(step):
        for at in range(2):
            a_copy(0, 0, me, f_send.at[step, at]).wait_send()
        a_copy(0, 0, me, g_send.at[step]).wait_send()

    for yy in range(2):
        @pl.when(branch == 0)
        def _():
            for pair in range(2):
                h_copy(2 * yy + pair).wait_send()


def per_device(
    query_rows, key_rows, value_rows, residual, control_mask, step_index, step_gates, out_weight
):
    rows = query_rows.shape[1]
    tokens = rows * SEQ
    block = 2 * rows
    steps = tokens // block
    width = residual.shape[1]
    features = out_weight.shape[1]
    wide = NZ * out_weight.shape[2] + 64
    weight_rows = jnp.swapaxes(out_weight[0], 0, 1)
    bf16, f32 = jnp.bfloat16, jnp.float32
    hbm = pl.BlockSpec(memory_space=pl.ANY)
    dma = pltpu.SemaphoreType.DMA
    block_out = pl.pallas_call(
        fused_kernel,
        out_shape=jax.ShapeDtypeStruct((rows, width), bf16),
        in_specs=[pl.BlockSpec(memory_space=pltpu.SMEM)] + [hbm] * 7,
        out_specs=pl.BlockSpec(memory_space=pltpu.VMEM),
        scratch_shapes=[
            pltpu.VMEM((tokens, DH), bf16),
            pltpu.VMEM((tokens, DH), bf16),
            pltpu.VMEM((tokens, 2 * DH), bf16),
            pltpu.VMEM((block, tokens), f32),
            pltpu.VMEM((block, tokens), f32),
            pltpu.VMEM((block, DH), f32),
            pltpu.VMEM((block, DH), f32),
            pltpu.VMEM((steps, block, DH), bf16),
            pltpu.VMEM((NX * rows, features), bf16),
            pltpu.VMEM((2 * wide, features), bf16),
            pltpu.VMEM((NX * rows, 2 * wide), bf16),
            pltpu.VMEM((NX, rows, 2 * wide), bf16),
            pltpu.VMEM((4, rows, width // 4), bf16),
            pltpu.VMEM((rows, width), bf16),
            pltpu.VMEM((rows, 1), jnp.int32),
            pltpu.VMEM(step_gates.shape, f32),
            dma((3, SEQ)), dma((3, SEQ)), dma((9,)), dma((28,)), dma((2, NZ, 4)),
            dma((steps,)), dma((SEQ, 2)), dma((steps, 2)), dma((steps,)),
            dma((3, NX)), dma((3, NX)), dma((4,)), dma((4,)),
        ],
        compiler_params=pltpu.CompilerParams(
            collective_id=0, has_side_effects=True, vmem_limit_bytes=60000 * 1024
        ),
        name="attend_project",
    )(
        step_index, query_rows, key_rows, value_rows, weight_rows, residual,
        control_mask[:, None], step_gates,
    )
    return block_out[None]


def solution(mesh):
    placed = (
        P("branch", ("group", "seq"), None),
        P("branch", ("group", "seq"), None),
        P("branch", ("group", "seq"), None),
        P(("group", "seq"), None),
        P(("group", "seq")),
        P("group"),
        P(),
        P("branch", None, "seq"),
    )
    return jax.shard_map(
        per_device,
        mesh=mesh,
        in_specs=placed,
        out_specs=P("branch", ("group", "seq"), None),
        check_vma=False,
    )
```
